1024 devices in a mesh: section: 16 (over x, z_hi), expert: 64 (over y, z_lo, core).
Axes of the slice: x: 4, y: 8, z: 16 (z_hi: 4, z_lo: 4; z = z_hi * 4 + z_lo), core: 2. Of those that a mesh axis runs over, the one named last changes fastest.
Arguments:
- tokens_a: bfloat16 [1024, 3584], P('expert'), may hold values from -6 to 6
- routes_a: int32 [1024, 8], P('expert'), may hold values from 0 to 63, as said below
- gates_a: float32 [1024, 8], P('expert'), may hold values from 0.1 to 0.4
- cotangent_b: bfloat16 [1024, 3584], P('expert'), may hold values from -6 to 6
- routes_b: int32 [1024, 8], P('expert'), may hold values from 0 to 63, as said below
- gates_b: float32 [1024, 8], P('expert'), may hold values from 0.1 to 0.4
- gate_weight: bfloat16 [64, 3584, 2048], P('expert', None, 'section'), may hold values from -0.09375 to 0.09375
- up_weight: bfloat16 [64, 3584, 2048], P('expert', None, 'section'), may hold values from -0.09375 to 0.09375
- down_weight: bfloat16 [64, 2048, 3584], P('expert', 'section'), may hold values from -0.125 to 0.125
- saved_gate: bfloat16 [64, 192, 2048], P('expert', None, 'section'), may hold values from -6 to 6
- saved_up: bfloat16 [64, 192, 2048], P('expert', None, 'section'), may hold values from -6 to 6
Outputs:
- forward_out: bfloat16 [1024, 3584], P('expert', 'section')
- input_grad: bfloat16 [1024, 3584], P('expert', 'section')
The draws below stay inside these ranges and needn't reach their ends.
Inputs may be any that keep to these rules, and one draw needn't show every extreme that they name: `routes_a`: each row names 8 different experts. Within each aligned block of 16 rows no expert is named more than 3 times, and one expert, the same in every block, is named exactly 3 times in each block. `routes_b`: each row names 8 different experts. Within each aligned block of 16 rows no expert is named more than 3 times, and one expert, the same in every block, is named exactly 3 times in each block.
All inputs are finite; a program needn't handle non-finite values.
Results may differ from the reference program's by a relative error of at most 0.015.
Values may be sent and summed in bfloat16 or wider, within the bound.
A program may use at most 32 MiB of HBM per device.

```python
import jax
import jax.numpy as jnp
from jax import lax

D = 3584
FF = 2048
TOP = 8
TOK_DEV = 16
EXPERTS = 64
CAP = 3
SLOTS = 192
TOKENS = 1024
N_SECTION = 16
N_EXPERT = 64


def pick_routes(base_key):
    block_count = TOKENS // TOK_DEV
    busiest = jax.random.randint(jax.random.fold_in(base_key, 1), (), 0, EXPERTS).astype(jnp.int32)

    def one_block(block_key):
        pick_key, row_key, col_key = jax.random.split(block_key, 3)
        tickets = jnp.arange((EXPERTS - 1) * CAP, dtype=jnp.int32)
        chosen = jax.random.permutation(pick_key, tickets)[:TOK_DEV * TOP - CAP]
        others = chosen // CAP
        others = others + (others >= busiest).astype(jnp.int32)
        labels = jnp.concatenate([jnp.full((CAP,), busiest, jnp.int32), others])
        labels = jnp.sort(labels)
        route_table = labels.reshape(TOP, TOK_DEV).T
        route_table = route_table[jax.random.permutation(row_key, TOK_DEV)]
        return jax.random.permutation(col_key, route_table, axis=1, independent=True)
    block_keys = jax.random.split(jax.random.fold_in(base_key, 2), block_count)
    return jax.vmap(one_block)(block_keys).reshape(TOKENS, TOP).astype(jnp.int32)


def draw_routes_a(key, part):
    return pick_routes(jax.random.fold_in(key, 11))


def draw_routes_b(key, part):
    return pick_routes(jax.random.fold_in(key, 23))


def block_scale(own_key, extent, shards, low, largest):
    factor_of, own = 1.0, jax.random.fold_in(own_key, 6)
    for axis_at, parts in shards:
        draws = jnp.exp(jax.random.uniform(jax.random.fold_in(own, axis_at), (parts,), jnp.float32, low / len(shards), largest / len(shards)))
        factor_of = factor_of * jnp.repeat(draws, extent[axis_at] // parts).reshape([-1 if axis == axis_at else 1 for axis in range(len(extent))])
    return factor_of


def gaussian(stream_key, extent, deviation, most, cuts=(), kind=jnp.bfloat16):
    level = block_scale(stream_key, extent, cuts, -0.22, 0.18) if cuts else 1.0
    entries = jax.random.normal(stream_key, extent, jnp.float32) * deviation * level
    return jnp.minimum(jnp.maximum(entries, -most), most).astype(kind)


def setup_inputs(seed: int = 0) -> dict:
    arg_keys = jax.random.split(jax.random.key(seed), 12)
    return {
        "tokens_a": gaussian(arg_keys[0], (TOKENS, D), 1.0, 6.0, ((0, 64),)),
        "routes_a": draw_routes_a(jax.random.fold_in(arg_keys[11], 71), 0),
        "gates_a": jnp.clip(0.1 + 0.3 * jax.random.uniform(arg_keys[2], (TOKENS, TOP), jnp.float32) ** block_scale(arg_keys[2], (TOKENS, TOP), ((0, 64),), -0.2, 0.2), 0.1, 0.4),
        "cotangent_b": gaussian(arg_keys[3], (TOKENS, D), 1.0, 6.0, ((0, 64),)),
        "routes_b": draw_routes_b(jax.random.fold_in(arg_keys[11], 71), 0),
        "gates_b": jnp.clip(0.1 + 0.3 * jax.random.uniform(arg_keys[5], (TOKENS, TOP), jnp.float32) ** block_scale(arg_keys[5], (TOKENS, TOP), ((0, 64),), -0.2, 0.2), 0.1, 0.4),
        "gate_weight": gaussian(arg_keys[6], (EXPERTS, D, FF), D ** -0.5, 0.09375, ((0, 64), (2, 16))),
        "up_weight": gaussian(arg_keys[7], (EXPERTS, D, FF), D ** -0.5, 0.09375, ((0, 64), (2, 16))),
        "down_weight": gaussian(arg_keys[8], (EXPERTS, FF, D), FF ** -0.5, 0.125, ((0, 64), (1, 16))),
        "saved_gate": gaussian(arg_keys[9], (EXPERTS, SLOTS, FF), 1.0, 6.0, ((0, 64), (2, 16))),
        "saved_up": gaussian(arg_keys[10], (EXPERTS, SLOTS, FF), 1.0, 6.0, ((0, 64), (2, 16))),
    }


def route_slots(routes):
    flat_ids = routes.reshape(N_EXPERT, TOK_DEV * TOP)
    onehot = (flat_ids[:, :, None] == jnp.arange(EXPERTS, dtype=jnp.int32)).astype(jnp.int32)
    before = jnp.cumsum(onehot, axis=1) - onehot
    ranking = jnp.sum(before * onehot, axis=2)
    blocks = jnp.arange(N_EXPERT, dtype=jnp.int32)[:, None]
    return flat_ids, (blocks * CAP + ranking).astype(jnp.int32)


def slot_rows(values, routes):
    flat_ids, position = route_slots(routes)
    route_ids = jnp.arange(TOKENS * TOP, dtype=jnp.int32).reshape(N_EXPERT, TOK_DEV * TOP)
    slot_table = jnp.full((EXPERTS, SLOTS), TOKENS * TOP, jnp.int32).at[flat_ids, position].set(route_ids)
    padded = jnp.concatenate([values, jnp.zeros((1, D), values.dtype)], axis=0)
    return padded[slot_table], flat_ids, position


def shard_sum(blocks):
    rounded = lax.optimization_barrier(blocks.astype(jnp.bfloat16))
    return jnp.sum(rounded.astype(jnp.float32), axis=0).astype(jnp.bfloat16)


def expert_step(operands):
    rows_a, rows_b, w_gate, w_up, w_down, saved_g, saved_u = operands
    part_ff = FF // N_SECTION
    gate_pre = jnp.dot(rows_a, w_gate, preferred_element_type=jnp.float32)
    up_pre = jnp.dot(rows_a, w_up, preferred_element_type=jnp.float32)
    hidden = (jax.nn.silu(gate_pre) * up_pre).astype(jnp.bfloat16)
    hid_blocks = hidden.reshape(SLOTS, N_SECTION, part_ff).astype(jnp.float32)
    down_blocks = w_down.reshape(N_SECTION, part_ff, D).astype(jnp.float32)
    expert_y = shard_sum(jnp.einsum('snf,nfd->nsd', hid_blocks, down_blocks))
    grad_hidden = lax.dot_general(rows_b, w_down, (((1,), (1,)), ((), ())), preferred_element_type=jnp.float32)
    pre_gate = saved_g.astype(jnp.float32)
    pre_up = saved_u.astype(jnp.float32)
    squash = jax.nn.sigmoid(pre_gate)
    grad_up = (grad_hidden * (pre_gate * squash)).astype(jnp.bfloat16)
    grad_gate = (grad_hidden * pre_up * squash * (1.0 + pre_gate * (1.0 - squash))).astype(jnp.bfloat16)
    gate_blocks = w_gate.reshape(D, N_SECTION, part_ff).astype(jnp.float32)
    up_blocks = w_up.reshape(D, N_SECTION, part_ff).astype(jnp.float32)
    block_terms = jnp.einsum('snf,dnf->nsd', grad_gate.reshape(SLOTS, N_SECTION, part_ff).astype(jnp.float32), gate_blocks)
    block_terms = block_terms + jnp.einsum('snf,dnf->nsd', grad_up.reshape(SLOTS, N_SECTION, part_ff).astype(jnp.float32), up_blocks)
    expert_dx = shard_sum(block_terms)
    return expert_y, expert_dx


def reference(tokens_a, routes_a, gates_a, cotangent_b, routes_b, gates_b, gate_weight, up_weight, down_weight, saved_gate, saved_up):
    values_a = jnp.repeat(tokens_a, TOP, axis=0)
    scaled = (gates_b[:, :, None] * cotangent_b[:, None, :].astype(jnp.float32)).astype(jnp.bfloat16)
    values_b = scaled.reshape(TOKENS * TOP, D)
    rows_a, flat_a, position_a = slot_rows(values_a, routes_a)
    rows_b, flat_b, position_b = slot_rows(values_b, routes_b)
    expert_y, expert_dx = lax.map(expert_step, (rows_a, rows_b, gate_weight, up_weight, down_weight, saved_gate, saved_up))
    returned_y = expert_y[flat_a, position_a].reshape(TOKENS, TOP, D).astype(jnp.float32)
    returned_dx = expert_dx[flat_b, position_b].reshape(TOKENS, TOP, D).astype(jnp.float32)
    forward_out = jnp.sum(gates_a[:, :, None] * returned_y, axis=1).astype(jnp.bfloat16)
    input_grad = jnp.sum(returned_dx, axis=1).astype(jnp.bfloat16)
    return forward_out, input_grad
```

```python
import functools

import jax
import jax.numpy as jnp
from jax import lax
from jax.experimental import pallas as pl
from jax.experimental.pallas import tpu as pltpu
from jax.sharding import PartitionSpec as P

NX, NZH, NY, NZL, NC = 4, 4, 8, 4, 2
TOK, TOP, RANKS = 16, 8, 3
D, FFL, SLOTS = 3584, 128, 192
Q = D // NX
COLS = D // (NX * NZH)
GRP = NZL * NC * 2
CH = RANKS * GRP
ROWS = NY * CH
LAG = 2
BF, F32, I32 = jnp.bfloat16, jnp.float32, jnp.int32
NEAR = (0, 1, 7, 2, 6, 3, 5, 4)
FAR = (4, 3, 5, 2, 6, 1, 7, 0)
HOPS = (
    [(dz, dc, kind) for dz in (1, -1) for dc in (0, 1) for kind in (2, 0, 1)]
    + [(2, dc, kind) for dc in (0, 1) for kind in (2, 0)]
    + [(-2, dc, 1) for dc in (0, 1)]
    + [(0, 1, kind) for kind in (2, 0, 1)]
)
NT = (((1,), (1,)), ((), ()))


def dot(a, b):
    return jnp.dot(a, b, preferred_element_type=F32)


def dot_nt(a, b):
    return lax.dot_general(a, b, NT, preferred_element_type=F32)


def iota(shape, axis):
    return lax.broadcasted_iota(I32, shape, axis)


def flag(cond):
    return jnp.where(cond, 1.0, 0.0)


def flatten_routes(table):
    shape = (TOK, TOK * TOP)
    row, lane = iota(shape, 0), iota(shape, 1)
    out = jnp.zeros(shape, F32)
    for k in range(TOP):
        hit = (lane >> 3 == row) & ((lane & 7) == k)
        out = out + jnp.where(hit, table[:, k : k + 1], 0.0)
    return jnp.sum(out, axis=0, keepdims=True)


def kernel(
    tok_a, tok_b, routes_a, routes_b, gates_a, gates_b, w_gate, w_up, w_down, sv_gate, sv_up,
    out_a, out_b,
    wg, wu, wd, sg, su,
    meta, met, tok, sel_t, send_y, rows, acc, hid, part, f1, f2, red, ret, dense, other, fin_src, fin,
    w_sem, own_sem, d1_s, d1_r, d2_s, d2_r, x_s, x_r, f_s, f_r,
    a_s, a_r, b_s, b_r, c_s, c_r, e_s, e_r, z_s, z_r,
):
    sec, exp = lax.axis_index("section"), lax.axis_index("expert")
    x, zh = lax.div(sec, NZH), lax.rem(sec, NZH)
    y, zl, c = lax.div(exp, NZL * NC), lax.rem(lax.div(exp, NC), NZL), lax.rem(exp, NC)
    z = zh * NZL + zl

    def at(dx=0, dy=0, dz=0, dc=0):
        z2 = lax.rem(z + (dz + 16), NZH * NZL)
        x2, y2, c2 = lax.rem(x + (dx + NX), NX), lax.rem(y + (dy + NY), NY), lax.rem(c + dc, NC)
        return (x2 * NZH + lax.div(z2, NZL), (y2 * NZL + lax.rem(z2, NZL)) * NC + c2)

    def remote(src, dst, s_sem, r_sem, where):
        return pltpu.make_async_remote_copy(
            src_ref=src, dst_ref=dst, send_sem=s_sem, recv_sem=r_sem,
            device_id=where, device_id_type=pl.DeviceIdType.MESH,
        )

    def ahead(dy):
        return lax.rem(y + dy, NY)

    loads = [pltpu.make_async_copy(sv_gate.at[0], sg, w_sem.at[0]),
             pltpu.make_async_copy(sv_up.at[0], su, w_sem.at[1])]
    for q in range(NX):
        span = pl.ds(q * Q, Q)
        loads.append(pltpu.make_async_copy(w_gate.at[0, span, :], wg.at[q], w_sem.at[2 + q]))
        loads.append(pltpu.make_async_copy(w_up.at[0, span, :], wu.at[q], w_sem.at[6 + q]))
        loads.append(pltpu.make_async_copy(w_down.at[0, :, span], wd.at[q], w_sem.at[10 + q]))
    for load in loads:
        load.start()

    barrier = pltpu.get_barrier_semaphore()
    peers = [at(dx=1), at(dx=-1)] + [at(dy=d) for d in range(1, NY)]
    peers += [at(dz=d) for d in range(1, 16)]
    peers += [at(dz=d, dc=1) for d in (-2, -1, 0, 1, 2)]
    for peer in peers:
        pl.semaphore_signal(barrier, inc=1, device_id=peer, device_id_type=pl.DeviceIdType.MESH)

    meta[...] = jnp.zeros((8, TOK * TOP), F32)
    meta[0:1, :] = flatten_routes(routes_a[...].astype(F32))
    meta[1:2, :] = flatten_routes(routes_b[...].astype(F32))
    meta[2:3, :] = flatten_routes(gates_a[...])
    meta[3:4, :] = flatten_routes(gates_b[...])
    pl.semaphore_wait(barrier, len(peers))

    block = c * NZL + zl
    columns = pl.ds(pl.multiple_of(x * Q, 128), Q)

    def landing(blk, kind):
        if kind == 2:
            return met.at[blk]
        return tok.at[pl.ds(pl.multiple_of((blk * 2 + kind) * TOK, TOK), TOK), :]

    def source(kind):
        return meta if kind == 2 else (tok_a, tok_b)[kind].at[:, columns]

    gather = [
        remote(source(kind), landing(block, kind), d1_s.at[n], d1_r.at[n], at(dz=dz, dc=dc))
        for n, (dz, dc, kind) in enumerate(HOPS)
    ]
    for copy in gather:
        copy.start()
    own = [pltpu.make_async_copy(source(kind), landing(block, kind), own_sem.at[kind]) for kind in range(3)]
    for copy in own:
        copy.start()
    for copy in own:
        copy.wait()
    for copy in gather:
        copy.wait_recv()

    sq = (128, 128)
    row, lane = iota(sq, 0), iota(sq, 1)
    small = iota((GRP, 128), 0)
    route_g, gate_g = jnp.zeros((GRP, 128), F32), jnp.zeros((GRP, 128), F32)
    for g in range(GRP):
        route_g = jnp.where(small == g, met[g // 2, g % 2 : g % 2 + 1, :], route_g)
        gate_g = jnp.where(small == g, met[g // 2, 2 + g % 2 : 3 + g % 2, :], gate_g)
    route_t = jnp.concatenate([route_g] * NY, axis=0)
    gate_t = jnp.concatenate([gate_g] * NY, axis=0)
    expert_id = (((row >> 4) * NZL + zl) * NC + c).astype(F32)
    named = flag(route_t == expert_id)
    before = dot(named.astype(BF), flag(row < lane).astype(BF))
    wide, tall = (128, 256), (256, 128)
    spread = flag((iota(wide, 0) >> 3) == (iota(wide, 1) & 15)).astype(BF)
    spread_t = flag((iota(tall, 1) >> 3) == (iota(tall, 0) & 15)).astype(BF)
    same = (iota(wide, 0) & 15) == (iota(wide, 1) >> 4)
    same_t = (iota(tall, 1) & 15) == (iota(tall, 0) >> 4)
    of_b = (row & 1) == 1
    for r in range(RANKS):
        hit = jnp.where(before == float(r), named, 0.0)
        pick = jnp.where(same, dot(hit.astype(BF), spread), 0.0).astype(BF)
        weight = hit * gate_t
        gate_row = jnp.sum(weight, axis=1, keepdims=True)
        scale = jnp.where((iota((128, 1), 0) & 1) == 1, gate_row, 1.0)
        picked = (dot(pick, tok[...]) * scale).astype(BF)
        send_y[:, r * GRP : (r + 1) * GRP, :] = picked.reshape(NY, GRP, Q)
        weight = jnp.where(of_b, hit, weight)
        high = weight.astype(BF)
        low = (weight - high.astype(F32)).astype(BF)
        sel_t[0, r] = jnp.where(same_t, dot_nt(spread_t, high), 0.0).astype(BF)
        sel_t[1, r] = jnp.where(same_t, dot_nt(spread_t, low), 0.0).astype(BF)

    def y_copy(dy):
        return remote(send_y.at[ahead(dy)], rows.at[x, y], d2_s.at[dy], d2_r.at[NY - dy], at(dy=dy))

    def y_wait(dy):
        remote(send_y.at[ahead(dy)], rows.at[x, ahead(dy)], d2_s.at[dy], d2_r.at[dy], at(dy=dy)).wait_recv()

    mine = pltpu.make_async_copy(send_y.at[y], rows.at[x, y], own_sem.at[0])
    mine.start()
    y_copies = [y_copy(dy) for dy in NEAR[1:]]
    for copy in y_copies:
        copy.start()

    left, right = lax.rem(x + NX - 1, NX), lax.rem(x + 1, NX)
    opposite = lax.rem(x + 2, NX)
    x_copies, forwards = [], []

    def x_copy(side, i, quarter, yc):
        ref = rows.at[quarter, yc]
        return remote(ref, ref, x_s.at[side, i], x_r.at[side, i], at(dx=1 - 2 * side))

    def forward(i, quarter, yc):
        ref = rows.at[quarter, yc]
        return remote(ref, ref, f_s.at[i], f_r.at[i], at(dx=1 if i % 2 == 0 else -1))

    for i in range(NY + LAG):
        if i < NY:
            if i == 0:
                mine.wait()
            else:
                y_wait(NEAR[i])
            for side in range(2):
                copy = x_copy(side, i, x, ahead(NEAR[i]))
                copy.start()
                x_copies.append(copy)
        j = i - LAG
        if j >= 0:
            yj = ahead(NEAR[j])
            x_copy(0, j, left, yj).wait_recv()
            x_copy(1, j, right, yj).wait_recv()
            copy = forward(j, left if j % 2 == 0 else right, yj)
            copy.start()
            forwards.append(copy)

    for load in loads:
        load.wait()

    def project(step, quarter):
        block_rows = rows[quarter].reshape(ROWS, Q)
        for n, value in enumerate((dot(block_rows, wg[quarter]), dot(block_rows, wu[quarter]),
                                   dot_nt(block_rows, wd[quarter]))):
            if step:
                value = acc[n] + value
            acc[n] = value

    for step, quarter in enumerate((x, left, right)):
        project(step, quarter)

    tallrow = iota((ROWS, SLOTS), 0)
    chunk_of = (tallrow * 1366) >> 16
    inner = tallrow - chunk_of * CH
    slot = (chunk_of * (NZL * NC) + ((inner >> 1) & 3) * NC + ((inner >> 3) & 1)) * RANKS + (inner >> 4)
    place = flag(slot == iota((ROWS, SLOTS), 1)).astype(BF)
    pre_gate, pre_up = dot(place, sg[...]), dot(place, su[...])
    squash = 1.0 / (1.0 + jnp.exp(-pre_gate))

    for i in range(NY):
        forward(i, opposite, ahead(NEAR[i])).wait_recv()
    project(3, opposite)

    is_b = (iota((ROWS, FFL), 0) & 1) == 1
    gate_pre, up_pre, grad = acc[0], acc[1], acc[2]
    value = gate_pre / (1.0 + jnp.exp(-gate_pre)) * up_pre
    hid[0] = jnp.where(is_b, 0.0, value).astype(BF)
    grad_up = grad * (pre_gate * squash)
    grad_gate = grad * pre_up * squash * (1.0 + pre_gate * (1.0 - squash))
    hid[1] = jnp.where(is_b, grad_gate, 0.0).astype(BF)
    hid[2] = jnp.where(is_b, grad_up, 0.0).astype(BF)

    def expand(n, quarter):
        value = dot(hid[0], wd[quarter]) + dot_nt(hid[1], wg[quarter]) + dot_nt(hid[2], wu[quarter])
        part[n] = value.astype(BF).reshape(NY, CH, Q)

    sends = []

    def go(copy):
        copy.start()
        sends.append(copy)

    def first_copy(i, yc):
        return remote(part.at[2, yc], f1.at[yc], a_s.at[i], a_r.at[i], at(dx=1 if i % 2 == 0 else -1))

    def second_copy(side, i, yc):
        return remote(part.at[side, yc], f2.at[side, yc], b_s.at[side, i], b_r.at[side, i], at(dx=1 - 2 * side))

    expand(2, opposite)
    for i in range(NY):
        go(first_copy(i, ahead(FAR[i])))
    for side, quarter in enumerate((right, left)):
        expand(side, quarter)
        for i in range(NY):
            if i % 2 != side:
                go(second_copy(side, i, ahead(FAR[i])))
    for i in range(NY):
        yc, side = ahead(FAR[i]), i % 2
        first_copy(i, yc).wait_recv()
        part[side, yc] = (part[side, yc].astype(F32) + f1[yc].astype(F32)).astype(BF)
        go(second_copy(side, i, yc))
    expand(3, x)

    def back_copy(dy):
        return remote(red.at[ahead(dy)], ret.at[y], c_s.at[dy], c_r.at[NY - dy], at(dy=dy))

    for i in range(NY):
        yc, dy = ahead(FAR[i]), FAR[i]
        second_copy(0, i, yc).wait_recv()
        second_copy(1, i, yc).wait_recv()
        total = part[3, yc].astype(F32) + f2[0, yc].astype(F32) + f2[1, yc].astype(F32)
        if dy:
            red[yc] = total.astype(BF)
            go(back_copy(dy))
        else:
            ret[yc] = total.astype(BF)
    for dy in FAR[:-1]:
        remote(red.at[ahead(dy)], ret.at[ahead(dy)], c_s.at[dy], c_r.at[dy], at(dy=dy)).wait_recv()

    total = jnp.zeros((256, Q), F32)
    for r in range(RANKS):
        back = ret[:, r * GRP : (r + 1) * GRP, :].reshape(NY * GRP, Q)
        total = total + dot(sel_t[0, r], back) + dot(sel_t[1, r], back)
    dense[...] = total.astype(BF).reshape(NC, 128, Q)
    core_copy = remote(dense.at[1 - c], other, e_s.at[0], e_r.at[0], at(dc=1))
    core_copy.start()
    core_copy.wait_recv()
    both = dense[c].astype(F32) + other[...].astype(F32)
    for h in range(NZH):
        turned = both if h == 0 else pltpu.roll(both, Q - h * COLS, axis=1)
        fin_src[h] = turned[:, 0:256].astype(BF).reshape(NZL, 2 * TOK, 256)

    def z_copy(dz):
        z2 = lax.rem(z + dz, 16)
        return remote(fin_src.at[lax.div(z2, NZL), lax.rem(z2, NZL)], fin.at[dz], z_s.at[dz], z_r.at[dz], at(dz=dz))

    z_order = sorted(range(1, 16), key=lambda d: -min(d, 16 - d))
    z_copies = [z_copy(dz) for dz in z_order]
    for copy in z_copies:
        copy.start()
    result = fin_src[zh, zl].astype(F32)
    for dz in reversed(z_order):
        z_copy(dz).wait_recv()
        result = result + fin[dz].astype(F32)
    out_a[...] = result[0:TOK, 0:COLS].astype(BF)
    out_b[...] = result[TOK : 2 * TOK, 0:COLS].astype(BF)

    for copy in gather + y_copies + x_copies + forwards + sends + [core_copy] + z_copies:
        copy.wait_send()


def body(tokens_a, routes_a, gates_a, cotangent_b, routes_b, gates_b,
         gate_weight, up_weight, down_weight, saved_gate, saved_up):
    far, near = pl.BlockSpec(memory_space=pl.ANY), pl.BlockSpec(memory_space=pltpu.VMEM)
    dma = lambda *shape: pltpu.SemaphoreType.DMA(shape)
    vmem = lambda dtype, *shape: pltpu.VMEM(shape, dtype)
    out = jax.ShapeDtypeStruct((TOK, COLS), BF)
    hops = len(HOPS)
    return pl.pallas_call(
        kernel,
        out_shape=(out, out),
        in_specs=[far, far, near, near, near, near, far, far, far, far, far],
        out_specs=(near, near),
        scratch_shapes=[
            vmem(BF, NX, Q, FFL), vmem(BF, NX, Q, FFL), vmem(BF, NX, FFL, Q),
            vmem(BF, SLOTS, FFL), vmem(BF, SLOTS, FFL),
            vmem(F32, 8, 128), vmem(F32, NZL * NC, 8, 128), vmem(BF, 256, Q),
            vmem(BF, 2, RANKS, 256, 128), vmem(BF, NY, CH, Q), vmem(BF, NX, NY, CH, Q),
            vmem(F32, 3, ROWS, FFL), vmem(BF, 3, ROWS, FFL), vmem(BF, NX, NY, CH, Q),
            vmem(BF, NY, CH, Q), vmem(BF, 2, NY, CH, Q), vmem(BF, NY, CH, Q), vmem(BF, NY, CH, Q),
            vmem(BF, NC, 128, Q), vmem(BF, 128, Q),
            vmem(BF, NZH, NZL, 2 * TOK, 256), vmem(BF, 16, 2 * TOK, 256),
            dma(14), dma(3), dma(hops), dma(hops), dma(NY), dma(NY), dma(2, NY), dma(2, NY), dma(NY), dma(NY),
            dma(NY), dma(NY), dma(2, NY), dma(2, NY), dma(NY), dma(NY), dma(1), dma(1), dma(16), dma(16),
        ],
        compiler_params=pltpu.CompilerParams(
            collective_id=0, has_side_effects=True, vmem_limit_bytes=60 * 1024 * 1024
        ),
        name="routed_experts",
    )(tokens_a, cotangent_b, routes_a, routes_b, gates_a, gates_b,
      gate_weight, up_weight, down_weight, saved_gate, saved_up)


def solution(mesh):
    placed = (
        P("expert", None), P("expert", None), P("expert", None),
        P("expert", None), P("expert", None), P("expert", None),
        P("expert", None, "section"), P("expert", None, "section"), P("expert", "section", None),
        P("expert", None, "section"), P("expert", None, "section"),
    )
    return jax.shard_map(
        body, mesh=mesh, in_specs=placed,
        out_specs=(P("expert", "section"), P("expert", "section")), check_vma=False,
    )
```

```python
import functools

import jax
import jax.numpy as jnp
from jax import lax
from jax.experimental import pallas as pl
from jax.experimental.pallas import tpu as pltpu
from jax.sharding import PartitionSpec as P

NX, NZH, NY, NZL, NC = 4, 4, 8, 4, 2
TOK, TOP, RANKS = 16, 8, 3
D, FFL, SLOTS = 3584, 128, 192
Q = D // NX
COLS = D // (NX * NZH)
GRP = NZL * NC * 2
CH = RANKS * GRP
ROWS = NY * CH
HALF = NY // 2
BF, F32, I32 = jnp.bfloat16, jnp.float32, jnp.int32
NEAR = (0, 1, 7, 2, 6, 3, 5, 4)
POS = (0, 1, 3, 5, 7, 6, 4, 2)
CUTS = ((0, 512), (512, 384))
TURNS = ((0, 256, 0), (128, 384, 96), (384, 384, 64), (640, 256, 32))
HOPS = (
    [(dz, dc, kind) for dz in (1, -1) for dc in (0, 1) for kind in (2, 0, 1)]
    + [(2, dc, kind) for dc in (0, 1) for kind in (2, 0)]
    + [(-2, dc, 1) for dc in (0, 1)]
    + [(0, 1, kind) for kind in (2, 0, 1)]
)
NT = (((1,), (1,)), ((), ()))


def dot(a, b):
    return jnp.dot(a, b, preferred_element_type=F32)


def dot_nt(a, b):
    return lax.dot_general(a, b, NT, preferred_element_type=F32)


def iota(shape, axis):
    return lax.broadcasted_iota(I32, shape, axis)


def flag(cond):
    return jnp.where(cond, 1.0, 0.0)


def flatten_routes(table):
    shape = (TOP, TOK * TOP)
    row, lane = iota(shape, 0), iota(shape, 1)
    out = jnp.zeros(shape, F32)
    for t in range(TOK):
        hit = (lane >> 4 == row) & ((lane & 15) == t)
        out = out + jnp.where(hit, table[:, t : t + 1], 0.0)
    return jnp.sum(out, axis=0, keepdims=True)


def kernel(
    tok_a, tok_b, routes_a, routes_b, gates_a, gates_b, w_gate, w_up, w_down, sv_gate, sv_up,
    out,
    wg, wu, wd, sg, su,
    meta, met, tok, sel_t, send_y, rows, acc, hid, part, f1, f2, red, ret, dense, other, tot, fin_src, fin,
    w_sem, own_sem, d1_s, d1_r, d2_s, d2_r, x_s, x_r, f_s, f_r,
    a_s, a_r, b_s, b_r, c_s, c_r, e_s, e_r, z_s, z_r,
):
    sec, exp = lax.axis_index("section"), lax.axis_index("expert")
    x, zh = lax.div(sec, NZH), lax.rem(sec, NZH)
    y, zl, c = lax.div(exp, NZL * NC), lax.rem(lax.div(exp, NC), NZL), lax.rem(exp, NC)
    z = zh * NZL + zl

    def at(dx=0, dy=0, dz=0, dc=0):
        z2 = lax.rem(z + (dz + 16), NZH * NZL)
        x2, y2, c2 = lax.rem(x + (dx + NX), NX), lax.rem(y + (dy + NY), NY), lax.rem(c + dc, NC)
        return (x2 * NZH + lax.div(z2, NZL), (y2 * NZL + lax.rem(z2, NZL)) * NC + c2)

    def remote(src, dst, s_sem, r_sem, where):
        return pltpu.make_async_remote_copy(
            src_ref=src, dst_ref=dst, send_sem=s_sem, recv_sem=r_sem,
            device_id=where, device_id_type=pl.DeviceIdType.MESH,
        )

    barrier = pltpu.get_barrier_semaphore()
    peers = [at(dx=1), at(dx=-1)] + [at(dy=d) for d in range(1, NY)]
    peers += [at(dz=d) for d in range(1, 16)]
    peers += [at(dz=d, dc=1) for d in (-2, -1, 0, 1, 2)]
    for peer in peers:
        pl.semaphore_signal(barrier, inc=1, device_id=peer, device_id_type=pl.DeviceIdType.MESH)

    loads = [pltpu.make_async_copy(sv_gate.at[0], sg, w_sem.at[0]),
             pltpu.make_async_copy(sv_up.at[0], su, w_sem.at[1])]
    for q in range(NX):
        span = pl.ds(q * Q, Q)
        loads.append(pltpu.make_async_copy(w_gate.at[0, span, :], wg.at[q], w_sem.at[2 + q]))
        loads.append(pltpu.make_async_copy(w_up.at[0, span, :], wu.at[q], w_sem.at[6 + q]))
        loads.append(pltpu.make_async_copy(w_down.at[0, :, span], wd.at[q], w_sem.at[10 + q]))
    for load in loads:
        load.start()

    meta[...] = jnp.zeros((8, TOK * TOP), F32)
    meta[0:1, :] = flatten_routes(routes_a[...].astype(F32))
    meta[1:2, :] = flatten_routes(routes_b[...].astype(F32))
    meta[2:3, :] = flatten_routes(gates_a[...])
    meta[3:4, :] = flatten_routes(gates_b[...])
    pl.semaphore_wait(barrier, len(peers))

    block = c * NZL + zl
    columns = pl.ds(pl.multiple_of(x * Q, 128), Q)

    def landing(blk, kind):
        if kind == 2:
            return met.at[blk]
        return tok.at[pl.ds(pl.multiple_of((blk * 2 + kind) * TOK, TOK), TOK), :]

    def source(kind):
        return meta if kind == 2 else (tok_a, tok_b)[kind].at[:, columns]

    gather = [
        remote(source(kind), landing(block, kind), d1_s.at[n], d1_r.at[n], at(dz=dz, dc=dc))
        for n, (dz, dc, kind) in enumerate(HOPS)
    ]
    own = [pltpu.make_async_copy(source(kind), landing(block, kind), own_sem.at[kind]) for kind in range(3)]
    for meta_first in (True, False):
        for n, (_, _, kind) in enumerate(HOPS):
            if (kind == 2) == meta_first:
                gather[n].start()
    for copy in own:
        copy.start()
    for copy in own:
        copy.wait()
    for n, (_, _, kind) in enumerate(HOPS):
        if kind == 2:
            gather[n].wait_recv()

    sq = (128, 128)
    row, lane = iota(sq, 0), iota(sq, 1)
    small = iota((GRP, 128), 0)
    route_g, gate_g = jnp.zeros((GRP, 128), F32), jnp.zeros((GRP, 128), F32)
    for g in range(GRP):
        route_g = jnp.where(small == g, met[g // 2, g % 2 : g % 2 + 1, :], route_g)
        gate_g = jnp.where(small == g, met[g // 2, 2 + g % 2 : 3 + g % 2, :], gate_g)
    route_t = jnp.concatenate([route_g] * NY, axis=0)
    gate_t = jnp.concatenate([gate_g] * NY, axis=0)
    expert_id = (((((row >> 4) + y) & 7) * NZL + zl) * NC + c).astype(F32)
    named = flag(route_t == expert_id)
    before = dot(named.astype(BF), flag((row & 15) < (lane & 15)).astype(BF))
    wide, tall = (128, 256), (256, 128)
    spread = flag((iota(wide, 0) & 15) == (iota(wide, 1) & 15)).astype(BF)
    same = (iota(wide, 0) & 15) == (iota(wide, 1) >> 4)
    picks = []
    for r in range(RANKS):
        hit = jnp.where(before == float(r), named, 0.0)
        pick = jnp.where(same, dot(hit.astype(BF), spread), 0.0).astype(BF)
        gate_row = jnp.sum(hit * gate_t, axis=1, keepdims=True)
        picks.append((pick, jnp.where((iota((128, 1), 0) & 1) == 1, gate_row, 1.0)))

    for n, (_, _, kind) in enumerate(HOPS):
        if kind != 2:
            gather[n].wait_recv()
    for r in range(RANKS):
        pick, scale = picks[r]
        picked = (dot(pick, tok[...]) * scale).astype(BF)
        slab = slice(r * GRP, (r + 1) * GRP)
        rows[0, 0, slab, :] = picked[0:GRP]
        send_y[:, slab, :] = picked[GRP:].reshape(NY - 1, GRP, Q)

    def y_copy(d):
        return remote(send_y.at[d - 1], rows.at[0, POS[NY - d]], d2_s.at[d], d2_r.at[NY - d], at(dy=d))

    x_copies, forwards = [], []

    def x_copy(side, p):
        return remote(rows.at[0, p], rows.at[3 - 2 * side, p], x_s.at[side, p], x_r.at[side, p], at(dx=1 - 2 * side))

    def forward(p):
        return remote(rows.at[3 if p % 2 == 0 else 1, p], rows.at[2, p], f_s.at[p], f_r.at[p],
                      at(dx=1 if p % 2 == 0 else -1))

    def x_step(p):
        if p:
            y_copy(NY - NEAR[p]).wait_recv()
        for side in range(2):
            x_copies.append(x_copy(side, p))
            x_copies[-1].start()

    def x_forward(p):
        x_copy(0, p).wait_recv()
        x_copy(1, p).wait_recv()
        forwards.append(forward(p))
        forwards[-1].start()

    y_copies = [y_copy(d) for d in NEAR[1:]]
    for copy in y_copies:
        copy.start()
    x_step(0)

    spread_t = flag((iota(tall, 1) & 15) == (iota(tall, 0) & 15)).astype(BF)
    same_t = (iota(tall, 1) & 15) == (iota(tall, 0) >> 4)
    of_b = (row & 1) == 1
    for r in range(RANKS):
        hit = jnp.where(before == float(r), named, 0.0)
        weight = jnp.where(of_b, hit, hit * gate_t)
        high = weight.astype(BF)
        low = (weight - high.astype(F32)).astype(BF)
        sel_t[0, r] = jnp.where(same_t, dot_nt(spread_t, high), 0.0).astype(BF)
        sel_t[1, r] = jnp.where(same_t, dot_nt(spread_t, low), 0.0).astype(BF)
    for load in loads:
        load.wait()

    mine = HALF * CH
    is_b = (iota((mine, FFL), 0) & 1) == 1

    def quarter(k):
        return lax.rem(x + k, NX)

    def project(h, k):
        block_rows = rows[k, h * HALF : (h + 1) * HALF].reshape(mine, Q)
        q = quarter(k)
        for n, value in enumerate((dot(block_rows, wg[q]), dot(block_rows, wu[q]), dot_nt(block_rows, wd[q]))):
            acc[n] = value if k == 0 else acc[n] + value

    def activate(h):
        at_row = iota((mine, SLOTS), 0)
        chunk = (at_row * 1366) >> 16
        inner = at_row - chunk * CH
        shift = jnp.full((mine, SLOTS), NEAR[h * HALF], I32)
        for i in range(1, HALF):
            shift = jnp.where(chunk == i, NEAR[h * HALF + i], shift)
        blk = ((shift + y) & 7) * (NZL * NC) + ((inner >> 1) & 3) * NC + ((inner >> 3) & 1)
        place = flag(blk * RANKS + (inner >> 4) == iota((mine, SLOTS), 1)).astype(BF)
        pre_gate, pre_up = dot(place, sg[...]), dot(place, su[...])
        squash = 1.0 / (1.0 + jnp.exp(-pre_gate))
        gate_pre, up_pre, grad = acc[0], acc[1], acc[2]
        value = gate_pre / (1.0 + jnp.exp(-gate_pre)) * up_pre
        hid[0] = jnp.where(is_b, 0.0, value).astype(BF)
        grad_up = grad * (pre_gate * squash)
        grad_gate = grad * pre_up * squash * (1.0 + pre_gate * (1.0 - squash))
        hid[1] = jnp.where(is_b, grad_gate, 0.0).astype(BF)
        hid[2] = jnp.where(is_b, grad_up, 0.0).astype(BF)

    def expand(h, k):
        q = quarter(k)
        value = dot(hid[0], wd[q]) + dot_nt(hid[1], wg[q]) + dot_nt(hid[2], wu[q])
        part[k, h * HALF : (h + 1) * HALF] = value.astype(BF).reshape(HALF, CH, Q)

    sends = []

    def go(copy):
        copy.start()
        sends.append(copy)

    def cols(s):
        return slice(CUTS[s][0], CUTS[s][0] + CUTS[s][1])

    def half(h):
        return range(h * HALF, (h + 1) * HALF)

    def first_copy(s, p):
        return remote(part.at[2, p, :, cols(s)], f1.at[p, :, cols(s)], a_s.at[s, p], a_r.at[s, p],
                      at(dx=1 if p % 2 == 0 else -1))

    def second_copy(s, side, p):
        return remote(part.at[1 + 2 * side, p, :, cols(s)], f2.at[side, p, :, cols(s)],
                      b_s.at[s, side, p], b_r.at[s, side, p], at(dx=1 - 2 * side))

    def send_first(s, h):
        for p in half(h):
            go(first_copy(s, p))

    def send_plain(s, h):
        for p in half(h):
            go(second_copy(s, 1 - p % 2, p))

    def send_added(s, h):
        for p in half(h):
            first_copy(s, p).wait_recv()
            k = 1 + 2 * (p % 2)
            total = part[k, p, :, cols(s)].astype(F32) + f1[p, :, cols(s)].astype(F32)
            part[k, p, :, cols(s)] = total.astype(BF)
            go(second_copy(s, p % 2, p))

    def back_copy(s, d):
        return remote(red.at[d, :, cols(s)], ret.at[(NY - d) % NY, :, cols(s)],
                      c_s.at[s, d], c_r.at[s, (NY - d) % NY], at(dy=d))

    def finish(s):
        for p in reversed(range(NY)):
            second_copy(s, 0, p).wait_recv()
            second_copy(s, 1, p).wait_recv()
            total = part[0, p, :, cols(s)].astype(F32) + f2[0, p, :, cols(s)].astype(F32)
            total = (total + f2[1, p, :, cols(s)].astype(F32)).astype(BF)
            d = NEAR[p]
            if d:
                red[d, :, cols(s)] = total
                go(back_copy(s, d))
            else:
                ret[0, :, cols(s)] = total

    def core_copy(s):
        return remote(dense.at[1 - c, :, cols(s)], other.at[:, cols(s)], e_s.at[s], e_r.at[s], at(dc=1))

    def combine(s):
        for d in range(1, NY):
            back_copy(s, NY - d).wait_recv()
        width = CUTS[s][1]
        total = jnp.zeros((256, width), F32)
        for r in range(RANKS):
            back = ret[:, r * GRP : (r + 1) * GRP, cols(s)].reshape(NY * GRP, width)
            total = total + dot(sel_t[0, r], back) + dot(sel_t[1, r], back)
        dense[:, :, cols(s)] = total.astype(BF).reshape(NC, 128, width)
        go(core_copy(s))

    def z_copy(zh2, zl2):
        behind = lax.rem(z + (16 - (zh2 * NZL + zl2)), 16)
        return remote(fin_src.at[zh2, zl2], fin.at[behind], z_s.at[zh2, zl2], z_r.at[behind],
                      (x * NZH + zh2, (y * NZL + zl2) * NC + c))

    def scatter(s):
        core_copy(s).wait_recv()
        tot[:, cols(s)] = dense[c, :, cols(s)].astype(F32) + other[:, cols(s)].astype(F32)
        for h in (2 * s, 2 * s + 1):
            base, width, shift = TURNS[h]
            turned = tot[:, base : base + width]
            if shift:
                turned = pltpu.roll(turned, width - shift, axis=1)
            fin_src[h] = turned[:, 0:256].astype(BF).reshape(NZL, 2 * TOK, 256)
        for h in (2 * s, 2 * s + 1):
            for l in range(NZL):
                @pl.when(z != h * NZL + l)
                def _():
                    z_copy(h, l).start()

    for p in range(HALF + 1):
        if p:
            x_step(p)
            x_forward(p - 1)
    for k in (0, 3, 1):
        project(0, k)
    for p in (5, 6):
        x_step(p)
        x_forward(p - 1)
    for p in half(0):
        forward(p).wait_recv()
    project(0, 2)
    activate(0)
    expand(0, 2)
    send_first(0, 0)
    for k in (1, 3):
        expand(0, k)
    send_plain(0, 0)
    x_step(7)
    x_forward(6)
    project(1, 0)
    send_added(0, 0)
    expand(0, 0)
    x_forward(7)
    for k in (3, 1):
        project(1, k)
    for p in half(1):
        forward(p).wait_recv()
    project(1, 2)
    activate(1)
    expand(1, 2)
    send_first(0, 1)
    for k in (1, 3):
        expand(1, k)
    send_plain(0, 1)
    send_first(1, 0)
    send_added(0, 1)
    send_first(1, 1)
    for h in range(2):
        send_plain(1, h)
    expand(1, 0)
    for h in range(2):
        send_added(1, h)
    finish(0)
    combine(0)
    scatter(0)
    finish(1)
    combine(1)
    scatter(1)

    result = fin_src[zh, zl].astype(F32)
    for behind in sorted(range(1, 16), key=lambda d: min(d, 16 - d)):
        remote(fin_src.at[0, 0], fin.at[behind], z_s.at[0, 0], z_r.at[behind], at(dz=1)).wait_recv()
        result = result + fin[behind].astype(F32)
    out[...] = result[:, 0:COLS].astype(BF)

    for copy in gather + y_copies + x_copies + forwards + sends:
        copy.wait_send()
    for h in range(NZH):
        for l in range(NZL):
            @pl.when(z != h * NZL + l)
            def _():
                z_copy(h, l).wait_send()


def body(tokens_a, routes_a, gates_a, cotangent_b, routes_b, gates_b,
         gate_weight, up_weight, down_weight, saved_gate, saved_up):
    far, near = pl.BlockSpec(memory_space=pl.ANY), pl.BlockSpec(memory_space=pltpu.VMEM)
    dma = lambda *shape: pltpu.SemaphoreType.DMA(shape)
    vmem = lambda dtype, *shape: pltpu.VMEM(shape, dtype)
    hops, mine = len(HOPS), HALF * CH
    both = pl.pallas_call(
        kernel,
        out_shape=jax.ShapeDtypeStruct((2 * TOK, COLS), BF),
        in_specs=[far, far, near, near, near, near, far, far, far, far, far],
        out_specs=near,
        scratch_shapes=[
            vmem(BF, NX, Q, FFL), vmem(BF, NX, Q, FFL), vmem(BF, NX, FFL, Q),
            vmem(BF, SLOTS, FFL), vmem(BF, SLOTS, FFL),
            vmem(F32, 8, 128), vmem(F32, NZL * NC, 8, 128), vmem(BF, 256, Q),
            vmem(BF, 2, RANKS, 256, 128), vmem(BF, NY - 1, CH, Q), vmem(BF, NX, NY, CH, Q),
            vmem(F32, 3, mine, FFL), vmem(BF, 3, mine, FFL), vmem(BF, NX, NY, CH, Q),
            vmem(BF, NY, CH, Q), vmem(BF, 2, NY, CH, Q), vmem(BF, NY, CH, Q), vmem(BF, NY, CH, Q),
            vmem(BF, NC, 128, Q), vmem(BF, 128, Q), vmem(F32, 128, Q),
            vmem(BF, NZH, NZL, 2 * TOK, 256), vmem(BF, 16, 2 * TOK, 256),
            dma(14), dma(3), dma(hops), dma(hops), dma(NY), dma(NY), dma(2, NY), dma(2, NY), dma(NY), dma(NY),
            dma(2, NY), dma(2, NY), dma(2, 2, NY), dma(2, 2, NY), dma(2, NY), dma(2, NY), dma(2), dma(2),
            dma(NZH, NZL), dma(16),
        ],
        compiler_params=pltpu.CompilerParams(
            collective_id=0, has_side_effects=True, vmem_limit_bytes=60 * 1024 * 1024
        ),
        name="routed_experts",
    )(tokens_a, cotangent_b, routes_a.T, routes_b.T, gates_a.T, gates_b.T,
      gate_weight, up_weight, down_weight, saved_gate, saved_up)
    return both[:TOK], both[TOK:]


def solution(mesh):
    placed = (
        P("expert", None), P("expert", None), P("expert", None),
        P("expert", None), P("expert", None), P("expert", None),
        P("expert", None, "section"), P("expert", None, "section"), P("expert", "section", None),
        P("expert", None, "section"), P("expert", None, "section"),
    )
    return jax.shard_map(
        body, mesh=mesh, in_specs=placed,
        out_specs=(P("expert", "section"), P("expert", "section")), check_vma=False,
    )
```

```python
import functools

import jax
import jax.numpy as jnp
from jax import lax
from jax.experimental import pallas as pl
from jax.experimental.pallas import tpu as pltpu
from jax.sharding import PartitionSpec as P

NX, NZH, NY, NZL, NC = 4, 4, 8, 4, 2
TOK, TOP, RANKS = 16, 8, 3
D, FFL, SLOTS = 3584, 128, 192
Q = D // NX
COLS = D // (NX * NZH)
GRP = NZL * NC * 2
CH = RANKS * GRP
ROWS = NY * CH
HALF = NY // 2
BF, F32, I32 = jnp.bfloat16, jnp.float32, jnp.int32
NEAR = (0, 1, 7, 2, 6, 3, 5, 4)
POS = (0, 1, 3, 5, 7, 6, 4, 2)
CUTS = ((0, 640), (640, 256), (0, 896))
MOVES = ((0, 0, 256), (256, 384, 384), (640, 256, 128), (768, 768, 128))
TURNS = (((0, 256),), ((128, 128), (640, 128), (256, 128)), ((256, 384),), ((512, 128), (768, 128)))
SHIFTS = (0, 96, 64, 32)
WAY = 512
HOPS = (
    [(dz, dc, kind) for dz in (1, -1) for dc in (0, 1) for kind in (2, 0, 1)]
    + [(2, dc, kind) for dc in (0, 1) for kind in (2, 0)]
    + [(-2, dc, 1) for dc in (0, 1)]
    + [(0, 1, kind) for kind in (2, 0, 1)]
)
NT = (((1,), (1,)), ((), ()))


def dot(a, b):
    return jnp.dot(a, b, preferred_element_type=F32)


def dot_nt(a, b):
    return lax.dot_general(a, b, NT, preferred_element_type=F32)


def iota(shape, axis):
    return lax.broadcasted_iota(I32, shape, axis)


def flag(cond):
    return jnp.where(cond, 1.0, 0.0)


def flatten_routes(table):
    shape = (TOP, TOK * TOP)
    row, lane = iota(shape, 0), iota(shape, 1)
    out = jnp.zeros(shape, F32)
    for t in range(TOK):
        hit = (lane >> 4 == row) & ((lane & 15) == t)
        out = out + jnp.where(hit, table[:, t : t + 1], 0.0)
    return jnp.sum(out, axis=0, keepdims=True)


def kernel(
    tok_a, tok_b, routes_a, routes_b, gates_a, gates_b, w_gate, w_up, w_down, sv_gate, sv_up,
    out,
    wg, wu, wd, sg, su,
    meta, met, tok, sel_t, send_y, rows, acc, hid, part, f1, f2, red, ret, dense, other, tot, fin_src, fin, hop_a, hop_b,
    w_sem, own_sem, d1_s, d1_r, d2_s, d2_r, x_s, x_r, f_s, f_r,
    a_s, a_r, b_s, b_r, c_s, c_r, e_s, e_r, z_s, z_r, h_s, h_r,
):
    sec, exp = lax.axis_index("section"), lax.axis_index("expert")
    x, zh = lax.div(sec, NZH), lax.rem(sec, NZH)
    y, zl, c = lax.div(exp, NZL * NC), lax.rem(lax.div(exp, NC), NZL), lax.rem(exp, NC)
    z = zh * NZL + zl

    def at(dx=0, dy=0, dz=0, dc=0):
        z2 = lax.rem(z + (dz + 16), NZH * NZL)
        x2, y2, c2 = lax.rem(x + (dx + NX), NX), lax.rem(y + (dy + NY), NY), lax.rem(c + dc, NC)
        return (x2 * NZH + lax.div(z2, NZL), (y2 * NZL + lax.rem(z2, NZL)) * NC + c2)

    def remote(src, dst, s_sem, r_sem, where):
        return pltpu.make_async_remote_copy(
            src_ref=src, dst_ref=dst, send_sem=s_sem, recv_sem=r_sem,
            device_id=where, device_id_type=pl.DeviceIdType.MESH,
        )

    barrier = pltpu.get_barrier_semaphore()
    peers = [at(dx=1), at(dx=-1)] + [at(dy=d) for d in range(1, NY)]
    peers += [at(dz=d) for d in range(1, 16)]
    peers += [at(dz=d, dc=1) for d in (-2, -1, 0, 1, 2)]
    for peer in peers:
        pl.semaphore_signal(barrier, inc=1, device_id=peer, device_id_type=pl.DeviceIdType.MESH)

    loads = [pltpu.make_async_copy(sv_gate.at[0], sg, w_sem.at[0]),
             pltpu.make_async_copy(sv_up.at[0], su, w_sem.at[1])]
    for q in range(NX):
        span = pl.ds(q * Q, Q)
        loads.append(pltpu.make_async_copy(w_gate.at[0, span, :], wg.at[q], w_sem.at[2 + q]))
        loads.append(pltpu.make_async_copy(w_up.at[0, span, :], wu.at[q], w_sem.at[6 + q]))
        loads.append(pltpu.make_async_copy(w_down.at[0, :, span], wd.at[q], w_sem.at[10 + q]))
    for load in loads:
        load.start()

    meta[...] = jnp.zeros((8, TOK * TOP), F32)
    meta[0:1, :] = flatten_routes(routes_a[...].astype(F32))
    meta[1:2, :] = flatten_routes(routes_b[...].astype(F32))
    meta[2:3, :] = flatten_routes(gates_a[...])
    meta[3:4, :] = flatten_routes(gates_b[...])
    pl.semaphore_wait(barrier, len(peers))

    block = c * NZL + zl
    columns = pl.ds(pl.multiple_of(x * Q, 128), Q)

    def landing(blk, kind):
        if kind == 2:
            return met.at[blk]
        return tok.at[pl.ds(pl.multiple_of((blk * 2 + kind) * TOK, TOK), TOK), :]

    def source(kind):
        return meta if kind == 2 else (tok_a, tok_b)[kind].at[:, columns]

    gather = [
        remote(source(kind), landing(block, kind), d1_s.at[n], d1_r.at[n], at(dz=dz, dc=dc))
        for n, (dz, dc, kind) in enumerate(HOPS)
    ]
    own = [pltpu.make_async_copy(source(kind), landing(block, kind), own_sem.at[kind]) for kind in range(3)]
    for meta_first in (True, False):
        for n, (_, _, kind) in enumerate(HOPS):
            if (kind == 2) == meta_first:
                gather[n].start()
    for copy in own:
        copy.start()
    own[2].wait()
    for n, (_, _, kind) in enumerate(HOPS):
        if kind == 2:
            gather[n].wait_recv()

    sq = (128, 128)
    row, lane = iota(sq, 0), iota(sq, 1)
    small = iota((GRP, 128), 0)
    route_g, gate_g = jnp.zeros((GRP, 128), F32), jnp.zeros((GRP, 128), F32)
    for g in range(GRP):
        route_g = jnp.where(small == g, met[g // 2, g % 2 : g % 2 + 1, :], route_g)
        gate_g = jnp.where(small == g, met[g // 2, 2 + g % 2 : 3 + g % 2, :], gate_g)
    route_t = jnp.concatenate([route_g] * NY, axis=0)
    gate_t = jnp.concatenate([gate_g] * NY, axis=0)
    expert_id = (((((row >> 4) + y) & 7) * NZL + zl) * NC + c).astype(F32)
    named = flag(route_t == expert_id)
    before = dot(named.astype(BF), flag((row & 15) < (lane & 15)).astype(BF))
    wide, tall = (128, 256), (256, 128)
    spread = flag((iota(wide, 0) & 15) == (iota(wide, 1) & 15)).astype(BF)
    same = (iota(wide, 0) & 15) == (iota(wide, 1) >> 4)
    picks = []
    for r in range(RANKS):
        hit = jnp.where(before == float(r), named, 0.0)
        pick = jnp.where(same, dot(hit.astype(BF), spread), 0.0).astype(BF)
        gate_row = jnp.sum(hit * gate_t, axis=1, keepdims=True)
        picks.append((pick, jnp.where((iota((128, 1), 0) & 1) == 1, gate_row, 1.0)))

    own[0].wait()
    own[1].wait()
    for n, (_, _, kind) in enumerate(HOPS):
        if kind != 2:
            gather[n].wait_recv()
    for r in range(RANKS):
        pick, scale = picks[r]
        picked = (dot(pick, tok[...]) * scale).astype(BF)
        slab = slice(r * GRP, (r + 1) * GRP)
        rows[0, 0, slab, :] = picked[0:GRP]
        send_y[:, slab, :] = picked[GRP:].reshape(NY - 1, GRP, Q)

    def y_copy(d):
        near = slice(0, WAY) if d == HALF else slice(0, Q)
        return remote(send_y.at[d - 1, :, near], rows.at[0, POS[NY - d], :, near], d2_s.at[d], d2_r.at[NY - d], at(dy=d))

    def detour():
        return remote(send_y.at[HALF - 1, :, WAY:Q], hop_a, d2_s.at[0], h_r.at[0], at(dy=-1))

    def pass_on():
        return remote(hop_a, rows.at[0, POS[HALF], :, WAY:Q], h_s.at[0], d2_r.at[0], at(dy=-3))

    x_copies, forwards, sends = [], [], []

    def go(copy):
        copy.start()
        sends.append(copy)

    def x_copy(side, p):
        return remote(rows.at[0, p], rows.at[3 - 2 * side, p], x_s.at[side, p], x_r.at[side, p], at(dx=1 - 2 * side))

    def forward(p):
        return remote(rows.at[3 if p % 2 == 0 else 1, p], rows.at[2, p], f_s.at[p], f_r.at[p],
                      at(dx=1 if p % 2 == 0 else -1))

    def x_step(p):
        if p:
            y_copy(NY - NEAR[p]).wait_recv()
        if NEAR[p] == HALF:
            pass_on().wait_recv()
        for side in range(2):
            x_copies.append(x_copy(side, p))
            x_copies[-1].start()

    def x_forward(p):
        x_copy(0, p).wait_recv()
        x_copy(1, p).wait_recv()
        forwards.append(forward(p))
        forwards[-1].start()

    y_copies = [y_copy(1), y_copy(7), detour()] + [y_copy(d) for d in NEAR[3:]]
    for copy in y_copies:
        copy.start()
    x_step(0)

    spread_t = flag((iota(tall, 1) & 15) == (iota(tall, 0) & 15)).astype(BF)
    same_t = (iota(tall, 1) & 15) == (iota(tall, 0) >> 4)
    of_b = (row & 1) == 1
    for r in range(RANKS):
        hit = jnp.where(before == float(r), named, 0.0)
        weight = jnp.where(of_b, hit, hit * gate_t)
        high = weight.astype(BF)
        low = (weight - high.astype(F32)).astype(BF)
        sel_t[0, r] = jnp.where(same_t, dot_nt(spread_t, high), 0.0).astype(BF)
        sel_t[1, r] = jnp.where(same_t, dot_nt(spread_t, low), 0.0).astype(BF)
    for load in loads:
        load.wait()

    mine = HALF * CH
    is_b = (iota((mine, FFL), 0) & 1) == 1

    def quarter(k):
        return lax.rem(x + k, NX)

    def project(h, k):
        block_rows = rows[k, h * HALF : (h + 1) * HALF].reshape(mine, Q)
        q = quarter(k)
        for n, value in enumerate((dot(block_rows, wg[q]), dot(block_rows, wu[q]), dot_nt(block_rows, wd[q]))):
            acc[n] = value if k == 0 else acc[n] + value

    def activate(h):
        at_row = iota((mine, SLOTS), 0)
        chunk = (at_row * 1366) >> 16
        inner = at_row - chunk * CH
        shift = jnp.full((mine, SLOTS), NEAR[h * HALF], I32)
        for i in range(1, HALF):
            shift = jnp.where(chunk == i, NEAR[h * HALF + i], shift)
        blk = ((shift + y) & 7) * (NZL * NC) + ((inner >> 1) & 3) * NC + ((inner >> 3) & 1)
        place = flag(blk * RANKS + (inner >> 4) == iota((mine, SLOTS), 1)).astype(BF)
        pre_gate, pre_up = dot(place, sg[...]), dot(place, su[...])
        squash = 1.0 / (1.0 + jnp.exp(-pre_gate))
        gate_pre, up_pre, grad = acc[0], acc[1], acc[2]
        value = gate_pre / (1.0 + jnp.exp(-gate_pre)) * up_pre
        hid[0] = jnp.where(is_b, 0.0, value).astype(BF)
        grad_up = grad * (pre_gate * squash)
        grad_gate = grad * pre_up * squash * (1.0 + pre_gate * (1.0 - squash))
        hid[1] = jnp.where(is_b, grad_gate, 0.0).astype(BF)
        hid[2] = jnp.where(is_b, grad_up, 0.0).astype(BF)

    def expand(h, k):
        q = quarter(k)
        for to, base, width in MOVES:
            span = slice(base, base + width)
            value = dot(hid[0], wd[q, :, span]) + dot_nt(hid[1], wg[q, span, :]) + dot_nt(hid[2], wu[q, span, :])
            part[k, h * HALF : (h + 1) * HALF, :, to : to + width] = value.astype(BF).reshape(HALF, CH, width)

    def cols(s):
        return slice(CUTS[s][0], CUTS[s][0] + CUTS[s][1])

    def half(h):
        return reversed(range(h * HALF, (h + 1) * HALF))

    def first_copy(s, p):
        return remote(part.at[2, p, :, cols(s)], f1.at[p, :, cols(s)], a_s.at[s, p], a_r.at[s, p],
                      at(dx=1 if p % 2 == 0 else -1))

    def second_copy(s, side, p):
        return remote(part.at[1 + 2 * side, p, :, cols(s)], f2.at[side, p, :, cols(s)],
                      b_s.at[s, side, p], b_r.at[s, side, p], at(dx=1 - 2 * side))

    def send_first(s, h):
        for p in half(h):
            go(first_copy(s, p))

    def send_plain(s, h):
        for p in half(h):
            go(second_copy(s, 1 - p % 2, p))

    def send_added(s, h):
        for p in half(h):
            first_copy(s, p).wait_recv()
            k = 1 + 2 * (p % 2)
            total = part[k, p, :, cols(s)].astype(F32) + f1[p, :, cols(s)].astype(F32)
            part[k, p, :, cols(s)] = total.astype(BF)
            go(second_copy(s, p % 2, p))

    def back_copy(s, d):
        if s == 1 and d == HALF:
            return remote(red.at[d, :, cols(s)], hop_b, c_s.at[s, d], h_r.at[1], at(dy=-1))
        return remote(red.at[d, :, cols(s)], ret.at[(NY - d) % NY, :, cols(s)],
                      c_s.at[s, d], c_r.at[s, (NY - d) % NY], at(dy=d))

    def back_pass():
        return remote(hop_b, ret.at[HALF, :, cols(1)], h_s.at[1], c_r.at[1, HALF], at(dy=-3))

    def finish(s, h):
        for p in half(h):
            second_copy(s, 0, p).wait_recv()
            second_copy(s, 1, p).wait_recv()
            total = part[0, p, :, cols(s)].astype(F32) + f2[0, p, :, cols(s)].astype(F32)
            total = (total + f2[1, p, :, cols(s)].astype(F32)).astype(BF)
            d = NEAR[p]
            if d:
                red[d, :, cols(s)] = total
                go(back_copy(s, d))
            else:
                ret[0, :, cols(s)] = total

    def core_copy(s):
        return remote(dense.at[1 - c, :, cols(s)], other.at[:, cols(s)], e_s.at[s], e_r.at[s], at(dc=1))

    def combine(s):
        if s == 0:
            for p in range(1, HALF):
                back_copy(2, NEAR[p]).wait_recv()
        for p in range(HALF, NY):
            if s == 1 and NEAR[p] == HALF:
                back_pass().wait_recv()
            else:
                back_copy(s, NEAR[p]).wait_recv()
        width = CUTS[s][1]
        total = jnp.zeros((256, width), F32)
        for r in range(RANKS):
            back = ret[:, r * GRP : (r + 1) * GRP, cols(s)].reshape(NY * GRP, width)
            total = total + dot(sel_t[0, r], back) + dot(sel_t[1, r], back)
        dense[:, :, cols(s)] = total.astype(BF).reshape(NC, 128, width)
        go(core_copy(s))

    def z_copy(zh2, zl2):
        behind = lax.rem(z + (16 - (zh2 * NZL + zl2)), 16)
        return remote(fin_src.at[zh2, zl2], fin.at[behind], z_s.at[zh2, zl2], z_r.at[behind],
                      (x * NZH + zh2, (y * NZL + zl2) * NC + c))

    def scatter(s):
        core_copy(s).wait_recv()
        tot[:, cols(s)] = dense[c, :, cols(s)].astype(F32) + other[:, cols(s)].astype(F32)
        for h in (s, s + 2):
            pieces = [tot[:, base : base + width] for base, width in TURNS[h]]
            turned = pieces[0] if len(pieces) == 1 else jnp.concatenate(pieces, axis=1)
            if SHIFTS[h]:
                turned = pltpu.roll(turned, turned.shape[1] - SHIFTS[h], axis=1)
            fin_src[h] = turned[:, 0:256].astype(BF).reshape(NZL, 2 * TOK, 256)
        for j in range(8):
            h = s + 2 * lax.rem(lax.div(zh, 2) + 1 + j // NZL, 2)
            l = lax.rem(zl + 2 + j, NZL)

            @pl.when(z != h * NZL + l)
            def _():
                z_copy(h, l).start()

    for p in range(1, HALF + 1):
        x_step(p)
        x_forward(p - 1)
        if p == 2:
            detour().wait_recv()
            go(pass_on())
    for k in (0, 3, 1):
        project(0, k)
    for p in (5, 6):
        x_step(p)
        x_forward(p - 1)
    for p in half(0):
        forward(p).wait_recv()
    project(0, 2)
    activate(0)
    expand(0, 2)
    send_first(2, 0)
    for k in (1, 3):
        expand(0, k)
    send_plain(2, 0)
    x_step(7)
    x_forward(6)
    project(1, 0)
    send_added(2, 0)
    expand(0, 0)
    x_forward(7)
    for k in (3, 1):
        project(1, k)
    for p in half(1):
        forward(p).wait_recv()
    project(1, 2)
    activate(1)
    expand(1, 2)
    send_first(0, 1)
    for k in (1, 3):
        expand(1, k)
    send_plain(0, 1)
    send_first(1, 1)
    finish(2, 0)
    send_added(0, 1)
    send_plain(1, 1)
    expand(1, 0)
    send_added(1, 1)
    finish(0, 1)
    finish(1, 1)
    back_copy(1, HALF).wait_recv()
    go(back_pass())
    combine(0)
    scatter(0)
    combine(1)
    scatter(1)

    result = fin_src[zh, zl].astype(F32)
    for behind in sorted(range(1, 16), key=lambda d: min(d, 16 - d)):
        remote(fin_src.at[0, 0], fin.at[behind], z_s.at[0, 0], z_r.at[behind], at(dz=1)).wait_recv()
        result = result + fin[behind].astype(F32)
    out[...] = result[:, 0:COLS].astype(BF)

    for copy in gather + y_copies + x_copies + forwards + sends:
        copy.wait_send()
    for h in range(NZH):
        for l in range(NZL):
            @pl.when(z != h * NZL + l)
            def _():
                z_copy(h, l).wait_send()


def body(tokens_a, routes_a, gates_a, cotangent_b, routes_b, gates_b,
         gate_weight, up_weight, down_weight, saved_gate, saved_up):
    far, near = pl.BlockSpec(memory_space=pl.ANY), pl.BlockSpec(memory_space=pltpu.VMEM)
    dma = lambda *shape: pltpu.SemaphoreType.DMA(shape)
    vmem = lambda dtype, *shape: pltpu.VMEM(shape, dtype)
    hops, mine = len(HOPS), HALF * CH
    both = pl.pallas_call(
        kernel,
        out_shape=jax.ShapeDtypeStruct((2 * TOK, COLS), BF),
        in_specs=[far, far, near, near, near, near, far, far, far, far, far],
        out_specs=near,
        scratch_shapes=[
            vmem(BF, NX, Q, FFL), vmem(BF, NX, Q, FFL), vmem(BF, NX, FFL, Q),
            vmem(BF, SLOTS, FFL), vmem(BF, SLOTS, FFL),
            vmem(F32, 8, 128), vmem(F32, NZL * NC, 8, 128), vmem(BF, 256, Q),
            vmem(BF, 2, RANKS, 256, 128), vmem(BF, NY - 1, CH, Q), vmem(BF, NX, NY, CH, Q),
            vmem(F32, 3, mine, FFL), vmem(BF, 3, mine, FFL), vmem(BF, NX, NY, CH, Q),
            vmem(BF, NY, CH, Q), vmem(BF, 2, NY, CH, Q), vmem(BF, NY, CH, Q), vmem(BF, NY, CH, Q),
            vmem(BF, NC, 128, Q), vmem(BF, 128, Q), vmem(F32, 128, Q),
            vmem(BF, NZH, NZL, 2 * TOK, 256), vmem(BF, 16, 2 * TOK, 256), vmem(BF, CH, Q - WAY), vmem(BF, CH, 256),
            dma(14), dma(3), dma(hops), dma(hops), dma(NY), dma(NY), dma(2, NY), dma(2, NY), dma(NY), dma(NY),
            dma(3, NY), dma(3, NY), dma(3, 2, NY), dma(3, 2, NY), dma(3, NY), dma(3, NY), dma(2), dma(2),
            dma(NZH, NZL), dma(16), dma(2), dma(2),
        ],
        compiler_params=pltpu.CompilerParams(
            collective_id=0, has_side_effects=True, vmem_limit_bytes=60 * 1024 * 1024
        ),
        name="routed_experts",
    )(tokens_a, cotangent_b, routes_a.T, routes_b.T, gates_a.T, gates_b.T,
      gate_weight, up_weight, down_weight, saved_gate, saved_up)
    return both[:TOK], both[TOK:]


def solution(mesh):
    placed = (
        P("expert", None), P("expert", None), P("expert", None),
        P("expert", None), P("expert", None), P("expert", None),
        P("expert", None, "section"), P("expert", None, "section"), P("expert", "section", None),
        P("expert", None, "section"), P("expert", None, "section"),
    )
    return jax.shard_map(
        body, mesh=mesh, in_specs=placed,
        out_specs=(P("expert", "section"), P("expert", "section")), check_vma=False,
    )
```

```python
import functools

import jax
import jax.numpy as jnp
from jax import lax
from jax.experimental import pallas as pl
from jax.experimental.pallas import tpu as pltpu
from jax.sharding import PartitionSpec as P

NX, NZH, NY, NZL, NC = 4, 4, 8, 4, 2
TOK, TOP, RANKS = 16, 8, 3
D, FFL, SLOTS = 3584, 128, 192
Q = D // NX
COLS = D // (NX * NZH)
GRP = NZL * NC * 2
CH = RANKS * GRP
ROWS = NY * CH
HALF = NY // 2
BF, F32, I32 = jnp.bfloat16, jnp.float32, jnp.int32
NEAR = (0, 1, 7, 2, 6, 3, 5, 4)
POS = (0, 1, 3, 5, 7, 6, 4, 2)
CUTS = ((0, 640), (640, 256), (0, 896))
MOVES = ((0, 0, 256), (256, 384, 384), (640, 256, 128), (768, 768, 128))
TURNS = (((0, 256),), ((128, 128), (640, 128), (256, 128)), ((256, 384),), ((512, 128), (768, 128)))
SHIFTS = (0, 96, 64, 32)
WAY = 512
HOPS = (
    [(dz, dc, kind) for dz in (1, -1) for dc in (0, 1) for kind in (2, 0, 1)]
    + [(2, dc, kind) for dc in (0, 1) for kind in (2, 0)]
    + [(-2, dc, 1) for dc in (0, 1)]
    + [(0, 1, kind) for kind in (2, 0, 1)]
)
NT = (((1,), (1,)), ((), ()))


def dot(a, b):
    return jnp.dot(a, b, preferred_element_type=F32)


def dot_nt(a, b):
    return lax.dot_general(a, b, NT, preferred_element_type=F32)


def iota(shape, axis):
    return lax.broadcasted_iota(I32, shape, axis)


def flag(cond):
    return jnp.where(cond, 1.0, 0.0)


def flatten_routes(table):
    shape = (TOP, TOK * TOP)
    row, lane = iota(shape, 0), iota(shape, 1)
    out = jnp.zeros(shape, F32)
    for t in range(TOK):
        hit = (lane >> 4 == row) & ((lane & 15) == t)
        out = out + jnp.where(hit, table[:, t : t + 1], 0.0)
    return jnp.sum(out, axis=0, keepdims=True)


def kernel(
    tok_a, tok_b, far_ra, far_rb, far_ga, far_gb, w_gate, w_up, w_down, sv_gate, sv_up,
    out,
    wg, wu, wd, sg, su,
    meta, met, tok, sel_t, send_y, rows, acc, hid, part, f1, f2, red, ret, dense, other, tot, fin_src, fin, hop_a, hop_b, routes_a, routes_b, gates_a, gates_b,
    w_sem, own_sem, d1_s, d1_r, d2_s, d2_r, x_s, x_r, f_s, f_r,
    a_s, a_r, b_s, b_r, c_s, c_r, e_s, e_r, z_s, z_r, h_s, h_r, t_sem,
):
    sec, exp = lax.axis_index("section"), lax.axis_index("expert")
    x, zh = lax.div(sec, NZH), lax.rem(sec, NZH)
    y, zl, c = lax.div(exp, NZL * NC), lax.rem(lax.div(exp, NC), NZL), lax.rem(exp, NC)
    z = zh * NZL + zl

    def at(dx=0, dy=0, dz=0, dc=0):
        z2 = lax.rem(z + (dz + 16), NZH * NZL)
        x2, y2, c2 = lax.rem(x + (dx + NX), NX), lax.rem(y + (dy + NY), NY), lax.rem(c + dc, NC)
        return (x2 * NZH + lax.div(z2, NZL), (y2 * NZL + lax.rem(z2, NZL)) * NC + c2)

    def remote(src, dst, s_sem, r_sem, where):
        return pltpu.make_async_remote_copy(
            src_ref=src, dst_ref=dst, send_sem=s_sem, recv_sem=r_sem,
            device_id=where, device_id_type=pl.DeviceIdType.MESH,
        )

    barrier = pltpu.get_barrier_semaphore()
    peers = [at(dx=1), at(dx=-1)] + [at(dy=d) for d in range(1, NY)]
    peers += [at(dz=d) for d in range(1, 16)]
    peers += [at(dz=d, dc=1) for d in (-2, -1, 0, 1, 2)]
    for peer in peers:
        pl.semaphore_signal(barrier, inc=1, device_id=peer, device_id_type=pl.DeviceIdType.MESH)

    tables = [pltpu.make_async_copy(src, dst, t_sem.at[n]) for n, (src, dst) in enumerate(
        ((far_ra, routes_a), (far_rb, routes_b), (far_ga, gates_a), (far_gb, gates_b)))]
    for copy in tables:
        copy.start()
    loads = [pltpu.make_async_copy(sv_gate.at[0], sg, w_sem.at[0]),
             pltpu.make_async_copy(sv_up.at[0], su, w_sem.at[1])]
    for q in range(NX):
        span = pl.ds(q * Q, Q)
        loads.append(pltpu.make_async_copy(w_gate.at[0, span, :], wg.at[q], w_sem.at[2 + q]))
        loads.append(pltpu.make_async_copy(w_up.at[0, span, :], wu.at[q], w_sem.at[6 + q]))
        loads.append(pltpu.make_async_copy(w_down.at[0, :, span], wd.at[q], w_sem.at[10 + q]))
    for load in loads:
        load.start()

    for copy in tables:
        copy.wait()
    meta[...] = jnp.zeros((8, TOK * TOP), F32)
    meta[0:1, :] = flatten_routes(routes_a[...].astype(F32))
    meta[1:2, :] = flatten_routes(routes_b[...].astype(F32))
    meta[2:3, :] = flatten_routes(gates_a[...])
    meta[3:4, :] = flatten_routes(gates_b[...])
    pl.semaphore_wait(barrier, len(peers))

    block = c * NZL + zl
    columns = pl.ds(pl.multiple_of(x * Q, 128), Q)

    def landing(blk, kind):
        if kind == 2:
            return met.at[blk]
        return tok.at[pl.ds(pl.multiple_of((blk * 2 + kind) * TOK, TOK), TOK), :]

    def source(kind):
        return meta if kind == 2 else (tok_a, tok_b)[kind].at[:, columns]

    gather = [
        remote(source(kind), landing(block, kind), d1_s.at[n], d1_r.at[n], at(dz=dz, dc=dc))
        for n, (dz, dc, kind) in enumerate(HOPS)
    ]
    own = [pltpu.make_async_copy(source(kind), landing(block, kind), own_sem.at[kind]) for kind in range(3)]
    for meta_first in (True, False):
        for n, (_, _, kind) in enumerate(HOPS):
            if (kind == 2) == meta_first:
                gather[n].start()
    for copy in own:
        copy.start()
    own[2].wait()
    for n, (_, _, kind) in enumerate(HOPS):
        if kind == 2:
            gather[n].wait_recv()

    sq = (128, 128)
    row, lane = iota(sq, 0), iota(sq, 1)
    small = iota((GRP, 128), 0)
    route_g, gate_g = jnp.zeros((GRP, 128), F32), jnp.zeros((GRP, 128), F32)
    for g in range(GRP):
        route_g = jnp.where(small == g, met[g // 2, g % 2 : g % 2 + 1, :], route_g)
        gate_g = jnp.where(small == g, met[g // 2, 2 + g % 2 : 3 + g % 2, :], gate_g)
    route_t = jnp.concatenate([route_g] * NY, axis=0)
    gate_t = jnp.concatenate([gate_g] * NY, axis=0)
    expert_id = (((((row >> 4) + y) & 7) * NZL + zl) * NC + c).astype(F32)
    named = flag(route_t == expert_id)
    before = dot(named.astype(BF), flag((row & 15) < (lane & 15)).astype(BF))
    wide, tall = (128, 256), (256, 128)
    spread = flag((iota(wide, 0) & 15) == (iota(wide, 1) & 15)).astype(BF)
    same = (iota(wide, 0) & 15) == (iota(wide, 1) >> 4)
    picks = []
    for r in range(RANKS):
        hit = jnp.where(before == float(r), named, 0.0)
        pick = jnp.where(same, dot(hit.astype(BF), spread), 0.0).astype(BF)
        gate_row = jnp.sum(hit * gate_t, axis=1, keepdims=True)
        picks.append((pick, jnp.where((iota((128, 1), 0) & 1) == 1, gate_row, 1.0)))

    own[0].wait()
    own[1].wait()
    for n, (_, _, kind) in enumerate(HOPS):
        if kind != 2:
            gather[n].wait_recv()
    for r in range(RANKS):
        pick, scale = picks[r]
        picked = (dot(pick, tok[...]) * scale).astype(BF)
        slab = slice(r * GRP, (r + 1) * GRP)
        rows[0, 0, slab, :] = picked[0:GRP]
        send_y[:, slab, :] = picked[GRP:].reshape(NY - 1, GRP, Q)

    def y_copy(d):
        near = slice(0, WAY) if d == HALF else slice(0, Q)
        return remote(send_y.at[d - 1, :, near], rows.at[0, POS[NY - d], :, near], d2_s.at[d], d2_r.at[NY - d], at(dy=d))

    def detour():
        return remote(send_y.at[HALF - 1, :, WAY:Q], hop_a, d2_s.at[0], h_r.at[0], at(dy=-1))

    def pass_on():
        return remote(hop_a, rows.at[0, POS[HALF], :, WAY:Q], h_s.at[0], d2_r.at[0], at(dy=-3))

    x_copies, forwards, sends = [], [], []

    def go(copy):
        copy.start()
        sends.append(copy)

    def x_copy(side, p):
        return remote(rows.at[0, p], rows.at[3 - 2 * side, p], x_s.at[side, p], x_r.at[side, p], at(dx=1 - 2 * side))

    def forward(p):
        return remote(rows.at[3 if p % 2 == 0 else 1, p], rows.at[2, p], f_s.at[p], f_r.at[p],
                      at(dx=1 if p % 2 == 0 else -1))

    def x_step(p):
        if p:
            y_copy(NY - NEAR[p]).wait_recv()
        if NEAR[p] == HALF:
            pass_on().wait_recv()
        for side in range(2):
            x_copies.append(x_copy(side, p))
            x_copies[-1].start()

    def x_forward(p):
        x_copy(0, p).wait_recv()
        x_copy(1, p).wait_recv()
        forwards.append(forward(p))
        forwards[-1].start()

    y_copies = [y_copy(1), y_copy(7), detour()] + [y_copy(d) for d in NEAR[3:]]
    for copy in y_copies:
        copy.start()
    x_step(0)

    spread_t = flag((iota(tall, 1) & 15) == (iota(tall, 0) & 15)).astype(BF)
    same_t = (iota(tall, 1) & 15) == (iota(tall, 0) >> 4)
    of_b = (row & 1) == 1
    for r in range(RANKS):
        hit = jnp.where(before == float(r), named, 0.0)
        weight = jnp.where(of_b, hit, hit * gate_t)
        high = weight.astype(BF)
        low = (weight - high.astype(F32)).astype(BF)
        sel_t[0, r] = jnp.where(same_t, dot_nt(spread_t, high), 0.0).astype(BF)
        sel_t[1, r] = jnp.where(same_t, dot_nt(spread_t, low), 0.0).astype(BF)
    for load in loads:
        load.wait()

    mine = HALF * CH
    is_b = (iota((mine, FFL), 0) & 1) == 1

    def quarter(k):
        return lax.rem(x + k, NX)

    def project(h, k):
        block_rows = rows[k, h * HALF : (h + 1) * HALF].reshape(mine, Q)
        q = quarter(k)
        for n, value in enumerate((dot(block_rows, wg[q]), dot(block_rows, wu[q]), dot_nt(block_rows, wd[q]))):
            acc[n] = value if k == 0 else acc[n] + value

    def activate(h):
        at_row = iota((mine, SLOTS), 0)
        chunk = (at_row * 1366) >> 16
        inner = at_row - chunk * CH
        shift = jnp.full((mine, SLOTS), NEAR[h * HALF], I32)
        for i in range(1, HALF):
            shift = jnp.where(chunk == i, NEAR[h * HALF + i], shift)
        blk = ((shift + y) & 7) * (NZL * NC) + ((inner >> 1) & 3) * NC + ((inner >> 3) & 1)
        place = flag(blk * RANKS + (inner >> 4) == iota((mine, SLOTS), 1)).astype(BF)
        pre_gate, pre_up = dot(place, sg[...]), dot(place, su[...])
        squash = 1.0 / (1.0 + jnp.exp(-pre_gate))
        gate_pre, up_pre, grad = acc[0], acc[1], acc[2]
        value = gate_pre / (1.0 + jnp.exp(-gate_pre)) * up_pre
        hid[0] = jnp.where(is_b, 0.0, value).astype(BF)
        grad_up = grad * (pre_gate * squash)
        grad_gate = grad * pre_up * squash * (1.0 + pre_gate * (1.0 - squash))
        hid[1] = jnp.where(is_b, grad_gate, 0.0).astype(BF)
        hid[2] = jnp.where(is_b, grad_up, 0.0).astype(BF)

    def expand(h, k):
        q = quarter(k)
        for to, base, width in MOVES:
            span = slice(base, base + width)
            value = dot(hid[0], wd[q, :, span]) + dot_nt(hid[1], wg[q, span, :]) + dot_nt(hid[2], wu[q, span, :])
            part[k, h * HALF : (h + 1) * HALF, :, to : to + width] = value.astype(BF).reshape(HALF, CH, width)

    def cols(s):
        return slice(CUTS[s][0], CUTS[s][0] + CUTS[s][1])

    def half(h):
        return reversed(range(h * HALF, (h + 1) * HALF))

    def first_copy(s, p):
        return remote(part.at[2, p, :, cols(s)], f1.at[p, :, cols(s)], a_s.at[s, p], a_r.at[s, p],
                      at(dx=1 if p % 2 == 0 else -1))

    def second_copy(s, side, p):
        return remote(part.at[1 + 2 * side, p, :, cols(s)], f2.at[side, p, :, cols(s)],
                      b_s.at[s, side, p], b_r.at[s, side, p], at(dx=1 - 2 * side))

    def send_first(s, h):
        for p in half(h):
            go(first_copy(s, p))

    def send_plain(s, h):
        for p in half(h):
            go(second_copy(s, 1 - p % 2, p))

    def send_added(s, h):
        for p in half(h):
            first_copy(s, p).wait_recv()
            k = 1 + 2 * (p % 2)
            total = part[k, p, :, cols(s)].astype(F32) + f1[p, :, cols(s)].astype(F32)
            part[k, p, :, cols(s)] = total.astype(BF)
            go(second_copy(s, p % 2, p))

    def back_copy(s, d):
        if s == 1 and d == HALF:
            return remote(red.at[d, :, cols(s)], hop_b, c_s.at[s, d], h_r.at[1], at(dy=-1))
        return remote(red.at[d, :, cols(s)], ret.at[(NY - d) % NY, :, cols(s)],
                      c_s.at[s, d], c_r.at[s, (NY - d) % NY], at(dy=d))

    def back_pass():
        return remote(hop_b, ret.at[HALF, :, cols(1)], h_s.at[1], c_r.at[1, HALF], at(dy=-3))

    def finish(s, h):
        for p in half(h):
            second_copy(s, 0, p).wait_recv()
            second_copy(s, 1, p).wait_recv()
            total = part[0, p, :, cols(s)].astype(F32) + f2[0, p, :, cols(s)].astype(F32)
            total = (total + f2[1, p, :, cols(s)].astype(F32)).astype(BF)
            d = NEAR[p]
            if d:
                red[d, :, cols(s)] = total
                go(back_copy(s, d))
            else:
                ret[0, :, cols(s)] = total

    def core_copy(s):
        return remote(dense.at[1 - c, :, cols(s)], other.at[:, cols(s)], e_s.at[s], e_r.at[s], at(dc=1))

    def combine(s):
        if s == 0:
            for p in range(1, HALF):
                back_copy(2, NEAR[p]).wait_recv()
        for p in range(HALF, NY):
            if s == 1 and NEAR[p] == HALF:
                back_pass().wait_recv()
            else:
                back_copy(s, NEAR[p]).wait_recv()
        width = CUTS[s][1]
        total = jnp.zeros((256, width), F32)
        for r in range(RANKS):
            back = ret[:, r * GRP : (r + 1) * GRP, cols(s)].reshape(NY * GRP, width)
            total = total + dot(sel_t[0, r], back) + dot(sel_t[1, r], back)
        dense[:, :, cols(s)] = total.astype(BF).reshape(NC, 128, width)
        go(core_copy(s))

    def z_copy(zh2, zl2):
        behind = lax.rem(z + (16 - (zh2 * NZL + zl2)), 16)
        return remote(fin_src.at[zh2, zl2], fin.at[behind], z_s.at[zh2, zl2], z_r.at[behind],
                      (x * NZH + zh2, (y * NZL + zl2) * NC + c))

    def scatter(s):
        core_copy(s).wait_recv()
        tot[:, cols(s)] = dense[c, :, cols(s)].astype(F32) + other[:, cols(s)].astype(F32)
        for h in (s, s + 2):
            pieces = [tot[:, base : base + width] for base, width in TURNS[h]]
            turned = pieces[0] if len(pieces) == 1 else jnp.concatenate(pieces, axis=1)
            if SHIFTS[h]:
                turned = pltpu.roll(turned, turned.shape[1] - SHIFTS[h], axis=1)
            fin_src[h] = turned[:, 0:256].astype(BF).reshape(NZL, 2 * TOK, 256)
        for j in range(8):
            h = s + 2 * lax.rem(lax.div(zh, 2) + 1 + j // NZL, 2)
            l = lax.rem(zl + 2 + j, NZL)

            @pl.when(z != h * NZL + l)
            def _():
                z_copy(h, l).start()

    for p in range(1, HALF + 1):
        x_step(p)
        x_forward(p - 1)
        if p == 2:
            detour().wait_recv()
            go(pass_on())
    for k in (0, 3, 1):
        project(0, k)
    for p in (5, 6, 7):
        x_step(p)
        x_forward(p - 1)
    for p in half(0):
        forward(p).wait_recv()
    project(0, 2)
    activate(0)
    expand(0, 2)
    send_first(2, 0)
    for k in (1, 3):
        expand(0, k)
    x_forward(7)
    send_plain(2, 0)
    for k in (0, 3, 1):
        project(1, k)
    send_added(2, 0)
    expand(0, 0)
    for p in half(1):
        forward(p).wait_recv()
    project(1, 2)
    activate(1)
    expand(1, 2)
    send_first(0, 1)
    for k in (1, 3):
        expand(1, k)
    send_plain(0, 1)
    send_first(1, 1)
    finish(2, 0)
    send_added(0, 1)
    send_plain(1, 1)
    expand(1, 0)
    send_added(1, 1)
    finish(0, 1)
    finish(1, 1)
    back_copy(1, HALF).wait_recv()
    go(back_pass())
    combine(0)
    scatter(0)
    combine(1)
    scatter(1)

    result = fin_src[zh, zl].astype(F32)
    for behind in sorted(range(1, 16), key=lambda d: min(d, 16 - d)):
        remote(fin_src.at[0, 0], fin.at[behind], z_s.at[0, 0], z_r.at[behind], at(dz=1)).wait_recv()
        result = result + fin[behind].astype(F32)
    out[...] = result[:, 0:COLS].astype(BF)

    for copy in gather + y_copies + x_copies + forwards + sends:
        copy.wait_send()
    for h in range(NZH):
        for l in range(NZL):
            @pl.when(z != h * NZL + l)
            def _():
                z_copy(h, l).wait_send()


def body(tokens_a, routes_a, gates_a, cotangent_b, routes_b, gates_b,
         gate_weight, up_weight, down_weight, saved_gate, saved_up):
    far, near = pl.BlockSpec(memory_space=pl.ANY), pl.BlockSpec(memory_space=pltpu.VMEM)
    dma = lambda *shape: pltpu.SemaphoreType.DMA(shape)
    vmem = lambda dtype, *shape: pltpu.VMEM(shape, dtype)
    hops, mine = len(HOPS), HALF * CH
    both = pl.pallas_call(
        kernel,
        out_shape=jax.ShapeDtypeStruct((2 * TOK, COLS), BF),
        in_specs=[far, far, far, far, far, far, far, far, far, far, far],
        out_specs=near,
        scratch_shapes=[
            vmem(BF, NX, Q, FFL), vmem(BF, NX, Q, FFL), vmem(BF, NX, FFL, Q),
            vmem(BF, SLOTS, FFL), vmem(BF, SLOTS, FFL),
            vmem(F32, 8, 128), vmem(F32, NZL * NC, 8, 128), vmem(BF, 256, Q),
            vmem(BF, 2, RANKS, 256, 128), vmem(BF, NY - 1, CH, Q), vmem(BF, NX, NY, CH, Q),
            vmem(F32, 3, mine, FFL), vmem(BF, 3, mine, FFL), vmem(BF, NX, NY, CH, Q),
            vmem(BF, NY, CH, Q), vmem(BF, 2, NY, CH, Q), vmem(BF, NY, CH, Q), vmem(BF, NY, CH, Q),
            vmem(BF, NC, 128, Q), vmem(BF, 128, Q), vmem(F32, 128, Q),
            vmem(BF, NZH, NZL, 2 * TOK, 256), vmem(BF, 16, 2 * TOK, 256), vmem(BF, CH, Q - WAY), vmem(BF, CH, 256),
            vmem(I32, TOP, TOK), vmem(I32, TOP, TOK), vmem(F32, TOP, TOK), vmem(F32, TOP, TOK),
            dma(14), dma(3), dma(hops), dma(hops), dma(NY), dma(NY), dma(2, NY), dma(2, NY), dma(NY), dma(NY),
            dma(3, NY), dma(3, NY), dma(3, 2, NY), dma(3, 2, NY), dma(3, NY), dma(3, NY), dma(2), dma(2),
            dma(NZH, NZL), dma(16), dma(2), dma(2), dma(4),
        ],
        compiler_params=pltpu.CompilerParams(
            collective_id=0, has_side_effects=True, vmem_limit_bytes=60 * 1024 * 1024
        ),
        name="routed_experts",
    )(tokens_a, cotangent_b, routes_a.T, routes_b.T, gates_a.T, gates_b.T,
      gate_weight, up_weight, down_weight, saved_gate, saved_up)
    return both[:TOK], both[TOK:]


def solution(mesh):
    placed = (
        P("expert", None), P("expert", None), P("expert", None),
        P("expert", None), P("expert", None), P("expert", None),
        P("expert", None, "section"), P("expert", None, "section"), P("expert", "section", None),
        P("expert", None, "section"), P("expert", None, "section"),
    )
    return jax.shard_map(
        body, mesh=mesh, in_specs=placed,
        out_specs=(P("expert", "section"), P("expert", "section")), check_vma=False,
    )
```
